128 devices in a mesh: leaf: 128 (over x, y, z, core).
Axes of the slice: x: 4, y: 4, z: 4, core: 2. Of those that a mesh axis runs over, the one named last changes fastest.
Arguments:
- points: bfloat16 [131072, 768], P('leaf'), may hold values from -4 to 4
- weights: bfloat16 [131072, 64], P('leaf'), may hold values from -0.0390625 to 0.0390625
- tree_slot: int32 [131072], P('leaf'), may hold values from 0 to 131071, as said below
- leaf_interp: bfloat16 [128, 256, 1024], P('leaf'), may hold values from -0.1875 to 0.1875
- skel_leaf: int32 [128, 256], P('leaf'), may hold values from 0 to 1023, as said below
- merge_interp: bfloat16 [128, 240, 512], P('leaf'), may hold values from -0.25 to 0.25
- merge_index: int32 [128, 240], P('leaf'), may hold values from 0 to 511, as said below
- near_mask: int32 [128, 8], P('leaf'), may hold values from 0 to 1, as said below
- far_mask: int32 [128, 4, 4], P('leaf'), may hold values from 0 to 1, as said below
Outputs:
- sums: float32 [131072, 64], P('leaf')
The draws below stay inside these ranges and needn't reach their ends.
Inputs may be any that keep to these rules, and one draw needn't show every extreme that they name: `tree_slot`: A permutation of the tree positions; each aligned block of 1024 input points sends exactly 8 points into the block of every leaf. `skel_leaf`: each row lists 256 distinct positions. `merge_index`: for every node of every level, the 256 entries of I_k are distinct. Symmetric: near_mask[l, 4 + s - 1] equals near_mask[l + s, 4 - s] for 1 <= s <= 4; entries that name a leaf outside the tree are 0. `far_mask`: entries that name a node outside its level are 0.
All inputs are finite; a program needn't handle non-finite values.
Results may differ from the reference program's by a relative error of at most 0.0042.
Values may be sent and summed in bfloat16 or wider, within the bound.
A program may use at most 128 MiB of HBM per device.

```python
import math
import jax
import jax.numpy as jnp
from jax import lax

D = 768
COLS = 64
RANK = 256
LEVELS = 4
NWIN = 4
FWIN = 2
PTS_DEV = 1024
POINTS = 131072
MROWS = 240
N_LEAF = 128


def draw_tree_slot(key, part):
    per_peer = PTS_DEV // N_LEAF
    leaf_ids = jnp.arange(N_LEAF, dtype=jnp.int32)
    source_key = jax.random.fold_in(key, 11)
    target_key = jax.random.fold_in(key, 12)
    source_perm = jax.vmap(lambda leaf_index: jax.random.permutation(jax.random.fold_in(source_key, leaf_index), PTS_DEV))(leaf_ids)
    target_perm = jax.vmap(lambda leaf_index: jax.random.permutation(jax.random.fold_in(target_key, leaf_index), PTS_DEV))(leaf_ids)
    rank_in = jnp.argsort(source_perm, axis=1).astype(jnp.int32)
    dest_leaf = rank_in // per_peer
    within_peer = rank_in % per_peer
    position = target_perm[dest_leaf, leaf_ids[:, None] * per_peer + within_peer]
    return (dest_leaf * PTS_DEV + position).reshape(-1).astype(jnp.int32)


def log_uniform(key, shape, low, high):
    return jnp.exp(jax.random.uniform(key, shape, jnp.float32, math.log(low), math.log(high)))


def draw_points(key, part):
    slots = draw_tree_slot(key, part)
    group_count = PTS_DEV // 4
    group_of = (slots % PTS_DEV // 4).astype(jnp.int32)
    point_count = slots.shape[0]
    centre_key = jax.random.fold_in(key, 7001)
    noise_key = jax.random.fold_in(key, 7002)
    spread_key = jax.random.fold_in(key, 7003)
    centres = 0.45 * jax.random.normal(centre_key, (group_count, D), jnp.float32)
    noise = jax.random.normal(noise_key, (point_count, D), jnp.float32)
    spread = log_uniform(spread_key, (point_count, 1), 0.05, 0.25)
    values = centres[group_of] + spread * noise
    return jnp.clip(values, -4.0, 4.0).astype(jnp.bfloat16)


def draw_skel_leaf(key, part):
    leaf_ids = jnp.arange(N_LEAF, dtype=jnp.int32)
    picked = jax.vmap(lambda leaf_index: jax.random.permutation(jax.random.fold_in(key, leaf_index), PTS_DEV)[:RANK])(leaf_ids)
    return picked.astype(jnp.int32)


def draw_merge_index(key, part):
    pieces = []
    for tree_level in range(1, LEVELS + 1):
        node_count = N_LEAF >> tree_level
        piece_rows = RANK >> tree_level
        level_key = jax.random.fold_in(key, 100 + tree_level)
        node_ids = jnp.arange(node_count, dtype=jnp.int32)
        picked = jax.vmap(lambda node_index: jax.random.permutation(jax.random.fold_in(level_key, node_index), 2 * RANK)[:RANK])(node_ids)
        pieces.append(picked.reshape(N_LEAF, piece_rows))
    return jnp.concatenate(pieces, axis=1).astype(jnp.int32)


def draw_near_mask(key, part):
    coin_flips = (jax.random.randint(key, (N_LEAF, NWIN), 0, 4) > 0).astype(jnp.int32)
    leaf_ids = jnp.arange(N_LEAF, dtype=jnp.int32)[:, None]
    distances = jnp.arange(1, NWIN + 1, dtype=jnp.int32)[None, :]
    upward = jnp.where(leaf_ids + distances < N_LEAF, coin_flips, 0)
    partner = jnp.clip(leaf_ids - distances, 0, N_LEAF - 1)
    column_ids = jnp.broadcast_to(distances - 1, partner.shape)
    downward = jnp.where(leaf_ids - distances >= 0, upward[partner, column_ids], 0)
    return jnp.concatenate([downward[:, ::-1], upward], axis=1).astype(jnp.int32)


def draw_far_mask(key, part):
    coin_flips = (jax.random.randint(key, (N_LEAF, LEVELS, 2 * FWIN), 0, 4) > 0).astype(jnp.int32)
    node_steps = jnp.concatenate([jnp.arange(-FWIN, 0, dtype=jnp.int32), jnp.arange(1, FWIN + 1, dtype=jnp.int32)])
    tree_levels = jnp.arange(1, LEVELS + 1, dtype=jnp.int32)
    leaf_ids = jnp.arange(N_LEAF, dtype=jnp.int32)
    node_ids = jnp.right_shift(leaf_ids[:, None, None], tree_levels[None, :, None]) + node_steps[None, None, :]
    limits = jnp.right_shift(jnp.full((LEVELS,), N_LEAF, jnp.int32), tree_levels)[None, :, None]
    valid = (node_ids >= 0) & (node_ids < limits)
    return jnp.where(valid, coin_flips, 0).astype(jnp.int32)


def steps_of(own_key, dims, cuts, least, high):
    def one(dim, blocks):
        heights = jax.random.uniform(jax.random.fold_in(jax.random.fold_in(own_key, 6), dim), (blocks,), jnp.float32, least / len(cuts), high / len(cuts))
        return jnp.repeat(jnp.exp(heights), dims[dim] // blocks).reshape((-1,) + (1,) * (len(dims) - dim - 1))

    gain = one(*cuts[0])
    for cut in cuts[1:]:
        gain = gain * one(*cut)
    return gain


def centred(own_key, extent, scale, reach, split=(), kind=jnp.bfloat16):
    drawn = scale * jax.random.normal(own_key, extent, jnp.float32)
    if split:
        drawn = drawn * steps_of(own_key, extent, split, -0.22, 0.18)
    return jnp.clip(drawn, -reach, reach).astype(kind)


def setup_inputs(seed: int = 0) -> dict:
    key_of = jax.random.split(jax.random.key(seed), 10)
    points = draw_points(jax.random.fold_in(key_of[9], 71), 0)
    weights = centred(key_of[1], (POINTS, COLS), 0.0065, 0.0390625, ((0, 128),))
    tree_slot = draw_tree_slot(jax.random.fold_in(key_of[9], 71), 0)
    leaf_interp = centred(key_of[3], (N_LEAF, RANK, PTS_DEV), PTS_DEV ** -0.5, 0.1875, ((0, 128),))
    skel_leaf = draw_skel_leaf(jax.random.fold_in(key_of[9], 71), 0)
    merge_interp = centred(key_of[5], (N_LEAF, MROWS, 2 * RANK), (2 * RANK) ** -0.5, 0.25, ((0, 128),))
    merge_index = draw_merge_index(jax.random.fold_in(key_of[9], 71), 0)
    near_mask = draw_near_mask(jax.random.fold_in(key_of[9], 71), 0)
    far_mask = draw_far_mask(jax.random.fold_in(key_of[9], 71), 0)
    return dict(points=points, weights=weights, tree_slot=tree_slot, leaf_interp=leaf_interp, skel_leaf=skel_leaf, merge_interp=merge_interp, merge_index=merge_index, near_mask=near_mask, far_mask=far_mask)


def row_offset(block, scale_inv):
    squares = lax.optimization_barrier(jnp.sum(jnp.square(block.astype(jnp.float32)), axis=1))
    return (squares - block.shape[1]) * (0.5 * scale_inv)

def kernel_block(targets, target_shift, sources, source_shift, scale_inv):
    products = jnp.dot(targets, sources.T, preferred_element_type=jnp.float32)
    exponent = products * scale_inv - target_shift[:, None] - source_shift[None, :]
    return jnp.exp(exponent).astype(jnp.bfloat16)

def kernel_sum(targets, target_shift, sources, source_weight, scale_inv):
    kernel = kernel_block(targets, target_shift, sources, row_offset(sources, scale_inv), scale_inv)
    return jnp.dot(kernel, source_weight, preferred_element_type=jnp.float32)

def reference(points, weights, tree_slot, leaf_interp, skel_leaf, merge_interp, merge_index, near_mask, far_mask):
    scale_inv = 1.0 / (1.75 * math.sqrt(D))
    source_of = jnp.argsort(tree_slot).astype(jnp.int32)
    leaf_points = points[source_of].reshape(N_LEAF, PTS_DEV, D)
    leaf_weights = weights[source_of].reshape(N_LEAF, PTS_DEV, COLS)
    pick_rows = jax.vmap(lambda block, chosen: block[chosen])
    skeleton = pick_rows(leaf_points, skel_leaf)
    skeleton_weight = jnp.einsum('lrp,lpc->lrc', leaf_interp.astype(jnp.float32), leaf_weights.astype(jnp.float32)).astype(jnp.bfloat16)
    level_points = []
    level_weights = []
    offset = 0
    for tree_level in range(1, LEVELS + 1):
        node_count = N_LEAF >> tree_level
        piece_rows = RANK >> tree_level
        both_points = skeleton.reshape(node_count, 2 * RANK, D)
        both_weights = skeleton_weight.reshape(node_count, 2 * RANK, COLS)
        interp = merge_interp[:, offset:offset + piece_rows].reshape(node_count, RANK, 2 * RANK)
        chosen = merge_index[:, offset:offset + piece_rows].reshape(node_count, RANK)
        skeleton = pick_rows(both_points, chosen)
        skeleton_weight = jnp.einsum('nrs,nsc->nrc', interp.astype(jnp.float32), both_weights.astype(jnp.float32)).astype(jnp.bfloat16)
        level_points.append(skeleton)
        level_weights.append(skeleton_weight)
        offset += piece_rows
    near_steps = list(range(-NWIN, 0)) + list(range(1, NWIN + 1))
    far_steps = list(range(-FWIN, 0)) + list(range(1, FWIN + 1))

    def one_leaf(leaf_id):
        own_points = leaf_points[leaf_id]
        own_weights = leaf_weights[leaf_id]
        own_shift = row_offset(own_points, scale_inv)

        def evaluate(operands):
            return kernel_sum(own_points, own_shift, operands[0], operands[1], scale_inv)

        def nothing(operands):
            return jnp.zeros((PTS_DEV, COLS), jnp.float32)
        outputs = evaluate((own_points, own_weights))
        for column, leaf_step in enumerate(near_steps):
            source_leaf = jnp.clip(leaf_id + leaf_step, 0, N_LEAF - 1)
            outputs = outputs + lax.cond(near_mask[leaf_id, column] > 0, evaluate, nothing, (leaf_points[source_leaf], leaf_weights[source_leaf]))
        for tree_level in range(1, LEVELS + 1):
            for column, node_step in enumerate(far_steps):
                node_id = jnp.clip(jnp.right_shift(leaf_id, tree_level) + node_step, 0, (N_LEAF >> tree_level) - 1)
                outputs = outputs + lax.cond(far_mask[leaf_id, tree_level - 1, column] > 0, evaluate, nothing, (level_points[tree_level - 1][node_id], level_weights[tree_level - 1][node_id]))
        return outputs
    tree_sums = lax.map(one_leaf, jnp.arange(N_LEAF, dtype=jnp.int32)).reshape(POINTS, COLS)
    return tree_sums[tree_slot]
```

```python
import math

import jax
import jax.numpy as jnp
from jax import lax
from jax.experimental import pallas as pl
from jax.experimental.pallas import tpu as pltpu
from jax.sharding import PartitionSpec as P

D = 768
W = 64
N = 1024
R = 256
LEAVES = 128
CHIPS = 64
GROUP = 16
PEER = N // LEAVES
MESSAGE = D + 128
MERGE = 240
PIECE = 2 * R + 128
F32 = jnp.float32
BF16 = jnp.bfloat16
SCALE = 1.0 / (1.75 * math.sqrt(D))
LOG2E = math.log2(math.e)
C_DOT = SCALE * LOG2E
C_SHIFT = 0.5 * SCALE * LOG2E
VMEM_LIMIT = 60 * 1024 * 1024
STEPS = (-2, -1, 1, 2)


def iota(shape, dim):
    return lax.broadcasted_iota(jnp.int32, shape, dim)


def one_hot(hit):
    return jnp.where(hit, 1.0, 0.0).astype(BF16)


def dot(a, b):
    return jnp.dot(a, b, preferred_element_type=F32)


def dot_nt(a, b):
    return lax.dot_general(a, b, (((1,), (1,)), ((), ())), preferred_element_type=F32)


def remote(src, dst, send, recv, device):
    return pltpu.make_async_remote_copy(
        src_ref=src,
        dst_ref=dst,
        send_sem=send,
        recv_sem=recv,
        device_id=(device,),
        device_id_type=pl.DeviceIdType.MESH,
    )


def greet(peers):
    barrier = pltpu.get_barrier_semaphore()
    for peer in peers:
        pl.semaphore_signal(
            barrier, inc=1, device_id=(peer,), device_id_type=pl.DeviceIdType.MESH
        )
    pl.semaphore_wait(barrier, len(peers))


def pack_kernel(slot_ref, pts_ref, tail_ref, piece_ref, send_ref, group_ref, send_sem, recv_sem):
    me = lax.axis_index("leaf")
    here = lax.rem(me, GROUP)
    base = me - here
    peers = [base + jnp.bitwise_xor(here, d) for d in range(1, GROUP)]
    greet(peers)
    copies = []
    for d in range(1, GROUP):
        first = 0 if d < 2 else 128 if d < 4 else 192 if d < 8 else 224
        rows = pl.ds(first, MERGE - first)
        copy = remote(
            piece_ref.at[rows],
            group_ref.at[here, rows],
            send_sem.at[d],
            recv_sem.at[d],
            peers[d - 1],
        )
        copy.start()
        copies.append(copy)
    group_ref[here] = piece_ref[...]

    row = slot_ref[...].astype(F32)
    col = jnp.transpose(jnp.broadcast_to(row, (8, N)))[:, 0:1]
    below = jnp.where(col < row, 1.0, 0.0)
    rank = jnp.sum(below, axis=0, keepdims=True).astype(jnp.int32)
    for i in range(4):
        rows = pl.ds(i * 256, 256)
        pick = one_hot(iota((256, N), 0) + i * 256 == rank)
        send_ref[rows, 0:D] = dot(pick, pts_ref[...]).astype(BF16)
        send_ref[rows, D:MESSAGE] = dot(pick, tail_ref[...]).astype(BF16)
    for copy in copies:
        copy.wait()


def unpack_kernel(slot_ref, home_ref, out_ref):
    row = slot_ref[...].astype(F32)
    col = jnp.transpose(jnp.broadcast_to(row, (8, N)))[:, 0:1]
    below = jnp.where(row < col, 1.0, 0.0)
    rank = jnp.sum(below, axis=1, keepdims=True).astype(jnp.int32)
    for i in range(4):
        pick = one_hot(iota((256, N), 1) == rank[i * 256 : (i + 1) * 256])
        both = dot(pick, home_ref[...])
        out_ref[pl.ds(i * 256, 256), :] = both[:, 0:W] + both[:, W : 2 * W]


class Copies:
    def __init__(self, send_sem, recv_sem):
        self.send_sem, self.recv_sem, self.all = send_sem, recv_sem, []

    def start(self, src, dst, device, recv=None):
        i = len(self.all)
        recv = i if recv is None else recv
        copy = remote(src, dst, self.send_sem.at[i], self.recv_sem.at[recv], device)
        copy.start()
        self.all.append(copy)
        return copy


COPIES = 80


def pick_lane(row, column):
    return jnp.sum(
        jnp.where(iota(row.shape, 1) == column, row, 0.0), axis=1, keepdims=True
    )


def tree_kernel(
    got, interp, skel_row, skel_col, mask_rows, group,
    out,
    xw, xv, mp, mw, mv, yp, yw, yv, rp, rw, rv,
    b1, b2, b3, b4, n4, far,
    pick_t, acol, ycol,
    xwt, ywt, mwt, rwx, rwy, xwm, mwm,
    acc_x, acc_y, acc_xt, acc_mt, acc_rt,
    ret_m, ret_y, ret_r, in_m, in_y, in_r,
    send_sem, recv_sem,
):
    me = lax.axis_index("leaf")
    chip = me // 2
    core = lax.rem(me, 2)
    mate = me + 1 - 2 * core

    def at(offset, which=None):
        other = lax.rem(chip + offset + CHIPS, CHIPS)
        return other * 2 + (core if which is None else which)

    right, left = at(1), at(-1)
    greet(
        [mate, at(1, 1 - core), at(-1, 1 - core)]
        + [at(o) for o in (1, -1, 2, -2, 4, -4, 8, -8, 16, -16)]
    )
    copies = Copies(send_sem, recv_sem)
    pts = got.at[:, pl.ds(0, D)]
    quarter = [pl.ds(256 * i, 256) for i in range(4)]

    mate_p = copies.start(pts, mp, mate)
    to_right, to_left = [], []

    def send_quarter(i):
        src = got.at[quarter[i], pl.ds(0, D)]
        to_left.append(copies.start(src, rp.at[core, quarter[i]], left))
        to_right.append(copies.start(src, yp.at[quarter[i]], right))

    send_quarter(0)

    lane = iota((1, 128), 1)
    for q in quarter:
        x = got[q, 0:D].astype(F32)
        acol[q, :] = (jnp.sum(x * x, axis=1, keepdims=True) - float(D)) * C_SHIFT
    a = acol[...]
    a_wide = jnp.broadcast_to(a, (N, 128))
    xv[...] = jnp.where(
        iota((8, N), 0) == 0, jnp.transpose(a_wide)[0:8], mask_rows[...]
    )
    tail = got[:, D:MESSAGE].astype(F32)
    place = (tail[:, W : W + 1] * 32.0 + tail[:, W + 1 : W + 2]).astype(jnp.int32)
    tail_t = jnp.transpose(tail)
    place_row = (tail_t[W : W + 1] * 32.0 + tail_t[W + 1 : W + 2]).astype(jnp.int32)
    high = a_wide.astype(BF16).astype(F32)
    middle = (a_wide - high).astype(BF16).astype(F32)
    low = a_wide - high - middle
    aux = jnp.where(lane == W, high, jnp.where(lane == W + 1, middle, low))
    aux = jnp.where((lane >= W) & (lane < W + 3), aux, 0.0).astype(BF16)
    pick_t[...] = one_hot(place == skel_row[...])
    own_pick = one_hot(skel_col[...] == place_row)
    tree_w = dot(one_hot(iota((N, N), 0) == place_row), got[:, D:MESSAGE]).astype(BF16)
    skel_w = dot(interp[...], tree_w)
    b1[core, :, 0:D] = dot(own_pick, got[:, 0:D]).astype(BF16)
    b1[core, :, D:MESSAGE] = jnp.where(lane < W, skel_w, dot(own_pick, aux)).astype(BF16)
    level0 = copies.start(b1.at[core], b1.at[core], mate)

    def merge(level, children, store):
        rows = R >> level
        first = R - 2 * rows
        here = lax.rem(me, GROUP)
        base = here - lax.rem(here, 1 << level)
        pieces = jnp.concatenate(
            [group[base + p, first : first + rows, :] for p in range(1 << level)], axis=0
        )
        index = pieces[:, 2 * R : 2 * R + 1].astype(F32) * 32.0
        index = index + pieces[:, 2 * R + 1 : 2 * R + 2].astype(F32)
        chosen = one_hot(index.astype(jnp.int32) == iota((R, 2 * R), 1))
        both = children[...].reshape(2 * R, MESSAGE)
        new_w = dot(pieces[:, 0 : 2 * R], both[:, D:MESSAGE])
        new = dot(chosen, both)
        new_tail = jnp.where(lane < W, new_w, new[:, D:MESSAGE]).astype(BF16)
        store[:, 0:D] = new[:, 0:D].astype(BF16)
        store[:, D:MESSAGE] = new_tail
        return chosen, new_tail

    half = pl.ds(pl.multiple_of(core * 128, 128), 128)

    def send_far(slot, offset, node):
        return [
            copies.start(node.at[half], far.at[slot + i, half], at(-step * offset))
            for i, step in enumerate(STEPS)
        ]

    def pass_on(copy, ref):
        copy.wait_recv()
        return copies.start(ref, ref, mate)

    x_t = jnp.transpose(tail)

    def block(tp, ta, tw_t, sp, sa, sw, acc_t, acc_s):
        k = dot_nt(tp, sp) * C_DOT
        k = jnp.exp2(k - ta - sa).astype(BF16)
        if acc_t is not None:
            acc_t[...] += dot(k, sw)
        if acc_s is not None:
            acc_s[...] += dot(tw_t, k)

    acc_x[...] = jnp.zeros_like(acc_x)
    acc_y[...] = jnp.zeros_like(acc_y)
    acc_xt[...] = jnp.zeros_like(acc_xt)
    acc_mt[...] = jnp.zeros_like(acc_mt)
    acc_rt[...] = jnp.zeros_like(acc_rt)
    mwt[...] = jnp.where(iota((128, 1), 0) < W, x_t, 0.0).astype(BF16)
    xwm[...] = jnp.where(lane < W, tail, 0.0).astype(BF16)

    def own_block(i):
        for j in range(i, 4):
            block(
                got[quarter[i], 0:D], acol[quarter[i], :], mwt[:, quarter[i]],
                got[quarter[j], 0:D], xv[0:1, quarter[j]], xwm[quarter[j], :],
                acc_x.at[quarter[i]], acc_xt.at[:, quarter[j]] if j > i else None,
            )

    own_block(0)

    level0.wait_recv()
    side2 = lax.rem(chip, 2)
    chosen, tail1 = merge(1, b1, b2.at[side2])
    level1 = copies.start(b2.at[side2, half], b2.at[side2, half], jnp.bitwise_xor(chip, 1) * 2 + core)
    send_quarter(1)
    mine = jnp.where(core == 0, chosen[:, 0:R].astype(F32), chosen[:, R : 2 * R].astype(F32))
    placed = dot_nt(pick_t[...], mine.astype(BF16)).astype(BF16)
    spread = pltpu.roll(dot(placed, tail1), W, 1)
    x_w = jnp.where(lane < W, tail, spread)
    xw[...] = x_w.astype(BF16)
    wv = []
    for src, dm, dl, dr in ((xw, mw, rw.at[core], yw), (xv, mv, rv.at[core], yv)):
        wv.append(
            (copies.start(src, dm, mate), copies.start(src, dl, left), copies.start(src, dr, right))
        )

    own_block(1)

    level1.wait_recv()
    other2 = b2.at[1 - side2, half]
    shared = copies.start(other2, other2, mate)
    own_block(2)
    own_block(3)
    shared.wait_recv()
    side3 = lax.rem(chip // 2, 2)
    merge(2, b2, b3.at[side3])
    level2 = copies.start(b3.at[side3, half], b3.at[side3, half], jnp.bitwise_xor(chip, 2) * 2 + core)
    far_copies = send_far(0, 2, b3.at[side3])
    send_quarter(2)

    mate_p.wait_recv()
    wv[0][0].wait_recv()
    wv[1][0].wait_recv()
    near_mate = pick_lane(xv[1:2, :], jnp.where(core == 0, 4, 3))
    mwm[...] = jnp.where(lane < W, mw[...].astype(F32) * near_mate, 0.0).astype(BF16)
    mwt[...] = (mwt[...].astype(F32) * near_mate).astype(BF16)

    def mate_block(h):
        for i in range(2):
            mine = pl.ds(h * 512 + i * 256, 256)
            theirs = pl.ds(pl.multiple_of(jnp.bitwise_xor(core, h) * 512, 512), 512)
            block(
                got[mine, 0:D], acol[mine, :], mwt[:, mine],
                mp[theirs, :], mv[0:1, theirs], mwm[theirs, :],
                acc_x.at[mine], acc_mt.at[:, theirs],
            )

    mate_block(0)
    level2.wait_recv()
    other3 = b3.at[1 - side3, half]
    shared = copies.start(other3, other3, mate)
    mate_block(1)
    ret_m[...] = acc_mt[0:W, :]
    back_m = copies.start(ret_m, in_m, mate)
    shared.wait_recv()
    side4 = lax.rem(chip // 4, 2)
    merge(3, b3, b4.at[side4])
    level3 = copies.start(b4.at[side4, half], b4.at[side4, half], jnp.bitwise_xor(chip, 4) * 2 + core)
    far_copies += send_far(4, 4, b4.at[side4])
    send_quarter(3)

    passed_w = [pass_on(wv[0][1], rw.at[core]), pass_on(wv[1][1], rv.at[core])]
    passed_p = [pass_on(to_left[0], rp.at[core, quarter[0]])]
    level3.wait_recv()
    other4 = b4.at[1 - side4, half]
    shared = copies.start(other4, other4, mate)
    wv[0][2].wait_recv()
    wv[1][2].wait_recv()
    y_row = jnp.broadcast_to(yv[0:1, :], (8, N))
    ycol[...] = jnp.transpose(y_row)[:, 0:1]
    y_w = yw[...].astype(F32)
    y_t = jnp.transpose(y_w)
    x_t = jnp.transpose(xw[...].astype(F32))
    shared.wait_recv()
    merge(4, b4, n4)
    far_copies += send_far(8, 8, n4)
    for copy in passed_w:
        copy.wait_recv()
    low_lane = lane < W
    low_row = iota((128, 1), 0) < W
    x_mask, y_mask = xv[1:2, :], yv[1:2, :]
    for j in range(2):
        r_mask = rv[j, 1:2, :]
        r_w = rw[j].astype(F32)
        step = 2 + j - core
        near = pick_lane(x_mask, step + 3)
        rwx[j] = (r_w * jnp.where(low_lane, near, pick_lane(x_mask, 8 + 2))).astype(BF16)
        xwt[j] = (x_t * jnp.where(low_row, near, pick_lane(r_mask, 8 + 1))).astype(BF16)
        step = 4 + j - core
        near = jnp.where(step <= 4, pick_lane(y_mask, step + 3), 0.0)
        rwy[j] = (r_w * jnp.where(low_lane, near, pick_lane(y_mask, 8 + 3))).astype(BF16)
        ywt[j] = (y_t * jnp.where(low_row, near, pick_lane(r_mask, 8 + 0))).astype(BF16)

    def near_quarter(i, tp, ta, tw_t, sw, acc):
        @pl.loop(0, 4)
        def _(t):
            rows = pl.ds(pl.multiple_of(t * 256, 256), 256)
            for j in range(2):
                block(
                    tp[rows, 0:D], ta[rows, :], tw_t[j, :, rows],
                    rp[j, quarter[i], :], rv[j, 0:1, quarter[i]], sw[j, quarter[i], :],
                    acc.at[rows], acc_rt.at[j, :, quarter[i]],
                )

    for i in range(4):
        passed_p[i].wait_recv()
        if i < 3:
            passed_p.append(pass_on(to_left[i + 1], rp.at[core, quarter[i + 1]]))
        near_quarter(i, got, acol, xwt, rwx, acc_x)
    for copy in to_right:
        copy.wait_recv()
    far_passed = []
    for i in range(4):
        for slot in range(3 * i, 3 * i + 3):
            far_passed.append(pass_on(far_copies[slot], far.at[slot, half]))
        near_quarter(i, yp, ycol, ywt, rwy, acc_y)
    y_sum = acc_y[:, 0:W] + acc_y[:, W : 2 * W]
    ret_y[...] = jnp.transpose(jnp.concatenate([y_sum, y_sum], axis=1))[0:W]
    ret_r[...] = acc_rt[:, 0:W, :] + acc_rt[:, W : 2 * W, :]
    back_y = copies.start(ret_y, in_y, left)
    for j in range(2):
        copies.start(ret_r.at[j], in_r.at[core], at(1, j), COPIES - 2 + core)

    for copy in far_passed:
        copy.wait_recv()

    @pl.loop(0, 12)
    def _(slot):
        mask = pick_lane(x_mask, 12 + slot)
        f_tail = far[slot, :, D:MESSAGE].astype(F32)
        f_w = jnp.where(low_lane, f_tail * mask, 0.0).astype(BF16)
        f_t = jnp.transpose(f_tail)
        f_a = f_t[W : W + 1] + f_t[W + 1 : W + 2] + f_t[W + 2 : W + 3]
        f_p = far[slot, :, 0:D]
        for t in range(4):
            block(
                got[quarter[t], 0:D], acol[quarter[t], :], None,
                f_p, f_a, f_w, acc_x.at[quarter[t]], None,
            )

    back_m.wait_recv()
    back_y.wait_recv()
    for j in range(2):
        remote(
            ret_r.at[j], in_r.at[j], send_sem.at[COPIES - 1], recv_sem.at[COPIES - 2 + j], left
        ).wait_recv()
    total = acc_xt[0:W, :] + in_m[...] + in_y[...] + in_r[0] + in_r[1]
    total = jnp.transpose(jnp.concatenate([total, total], axis=0))
    x_sum = acc_x[...]
    total = total + x_sum + pltpu.roll(x_sum, W, 1)
    high = total.astype(BF16).astype(F32)
    out[...] = jnp.where(lane < W, high, total - high).astype(BF16)
    for copy in copies.all:
        copy.wait_send()


def vmem(*shape, dtype=BF16):
    return pltpu.VMEM(shape, dtype)


def in_vmem(count):
    return [pl.BlockSpec(memory_space=pltpu.VMEM)] * count


def local(
    points, weights, tree_slot, leaf_interp, skel_leaf, merge_interp, merge_index, near_mask, far_mask
):
    slot_row = tree_slot.reshape(1, N)
    place = lax.rem(tree_slot, N)
    tail = jnp.concatenate(
        [
            weights,
            (place // 32).astype(BF16)[:, None],
            lax.rem(place, 32).astype(BF16)[:, None],
            jnp.zeros((N, 128 - W - 2), BF16),
        ],
        axis=1,
    )
    index = merge_index[0]
    piece = jnp.concatenate(
        [
            merge_interp[0],
            (index // 32).astype(BF16)[:, None],
            lax.rem(index, 32).astype(BF16)[:, None],
            jnp.zeros((MERGE, 126), BF16),
        ],
        axis=1,
    )
    mask_row = jnp.concatenate(
        [near_mask.reshape(1, 8), far_mask.reshape(1, 16)], axis=1
    ).astype(F32)
    mask_rows = jnp.pad(mask_row, ((1, 6), (0, N - 24)))
    send, group = pl.pallas_call(
        pack_kernel,
        out_shape=[
            jax.ShapeDtypeStruct((N, MESSAGE), BF16),
            jax.ShapeDtypeStruct((GROUP, MERGE, PIECE), BF16),
        ],
        in_specs=in_vmem(4),
        out_specs=in_vmem(2),
        scratch_shapes=[pltpu.SemaphoreType.DMA((GROUP,)), pltpu.SemaphoreType.DMA((GROUP,))],
        compiler_params=pltpu.CompilerParams(
            collective_id=0, has_side_effects=True, vmem_limit_bytes=VMEM_LIMIT
        ),
        name="pack",
    )(slot_row, points, tail, piece)
    got = lax.all_to_all(
        send.reshape(LEAVES, PEER, MESSAGE), "leaf", split_axis=0, concat_axis=0, tiled=True
    ).reshape(N, MESSAGE)
    sums = pl.pallas_call(
        tree_kernel,
        out_shape=jax.ShapeDtypeStruct((N, 128), BF16),
        in_specs=in_vmem(6),
        out_specs=pl.BlockSpec(memory_space=pltpu.VMEM),
        scratch_shapes=[
            vmem(N, 128), vmem(8, N, dtype=F32),
            vmem(N, D), vmem(N, 128), vmem(8, N, dtype=F32),
            vmem(N, D), vmem(N, 128), vmem(8, N, dtype=F32),
            vmem(2, N, D), vmem(2, N, 128), vmem(2, 8, N, dtype=F32),
            vmem(2, R, MESSAGE), vmem(2, R, MESSAGE), vmem(2, R, MESSAGE), vmem(2, R, MESSAGE),
            vmem(R, MESSAGE), vmem(12, R, MESSAGE),
            vmem(N, R), vmem(N, 1, dtype=F32), vmem(N, 1, dtype=F32),
            vmem(2, 128, N), vmem(2, 128, N), vmem(128, N),
            vmem(2, N, 128), vmem(2, N, 128), vmem(N, 128), vmem(N, 128),
            vmem(N, 128, dtype=F32), vmem(N, 128, dtype=F32),
            vmem(128, N, dtype=F32), vmem(128, N, dtype=F32), vmem(2, 128, N, dtype=F32),
            vmem(W, N, dtype=F32), vmem(W, N, dtype=F32), vmem(2, W, N, dtype=F32),
            vmem(W, N, dtype=F32), vmem(W, N, dtype=F32), vmem(2, W, N, dtype=F32),
            pltpu.SemaphoreType.DMA((COPIES,)), pltpu.SemaphoreType.DMA((COPIES,)),
        ],
        compiler_params=pltpu.CompilerParams(
            collective_id=1, has_side_effects=True, vmem_limit_bytes=VMEM_LIMIT
        ),
        name="tree",
    )(got, leaf_interp[0], skel_leaf, skel_leaf.reshape(R, 1), mask_rows, group)
    home = lax.all_to_all(
        sums.reshape(LEAVES, PEER, 128), "leaf", split_axis=0, concat_axis=0, tiled=True
    ).reshape(N, 128)
    return pl.pallas_call(
        unpack_kernel,
        out_shape=jax.ShapeDtypeStruct((N, W), F32),
        in_specs=in_vmem(2),
        out_specs=pl.BlockSpec(memory_space=pltpu.VMEM),
        compiler_params=pltpu.CompilerParams(vmem_limit_bytes=VMEM_LIMIT),
        name="unpack",
    )(slot_row, home)


def solution(mesh):
    placed = (
        P("leaf", None),
        P("leaf", None),
        P("leaf"),
        P("leaf", None, None),
        P("leaf", None),
        P("leaf", None, None),
        P("leaf", None),
        P("leaf", None),
        P("leaf", None, None),
    )
    return jax.shard_map(
        local, mesh=mesh, in_specs=placed, out_specs=P("leaf", None), check_vma=False
    )
```

```python
import math

import jax
import jax.numpy as jnp
from jax import lax
from jax.experimental import pallas as pl
from jax.experimental.pallas import tpu as pltpu
from jax.sharding import PartitionSpec as P

D = 768
W = 64
N = 1024
R = 256
LEAVES = 128
CHIPS = 64
GROUP = 16
PEER = N // LEAVES
MESSAGE = D + 128
MERGE = 240
F32 = jnp.float32
BF16 = jnp.bfloat16
SCALE = 1.0 / (1.75 * math.sqrt(D))
LOG2E = math.log2(math.e)
C_DOT = SCALE * LOG2E
C_SHIFT = 0.5 * SCALE * LOG2E
VMEM_LIMIT = 60 * 1024 * 1024


def iota(shape, dim):
    return lax.broadcasted_iota(jnp.int32, shape, dim)


def one_hot(hit):
    return jnp.where(hit, 1.0, 0.0).astype(BF16)


def dot(a, b):
    return jnp.dot(a, b, preferred_element_type=F32)


def dot_nt(a, b):
    return lax.dot_general(a, b, (((1,), (1,)), ((), ())), preferred_element_type=F32)


def remote(src, dst, send, recv, device):
    return pltpu.make_async_remote_copy(
        src_ref=src,
        dst_ref=dst,
        send_sem=send,
        recv_sem=recv,
        device_id=(device,),
        device_id_type=pl.DeviceIdType.MESH,
    )


class Copies:
    def __init__(self, send_sem, recv_sem):
        self.send_sem, self.recv_sem, self.all = send_sem, recv_sem, []

    def start(self, src, dst, device, recv=None):
        i = len(self.all)
        recv = i if recv is None else recv
        copy = remote(src, dst, self.send_sem.at[i], self.recv_sem.at[recv], device)
        copy.start()
        self.all.append(copy)
        return copy


COPIES = 160


def pick_lane(row, column):
    return jnp.sum(
        jnp.where(iota(row.shape, 1) == column, row, 0.0), axis=1, keepdims=True
    )


def column_of(row):
    return jnp.transpose(jnp.broadcast_to(row, (8, row.shape[1])))[:, 0:1]


def tree_kernel(
    slot, weights_t, points, interp, skel_row, merge_w, merge_i, near_mask, far_mask,
    out,
    send, came, got, tail_s, index, lines,
    xw, xv, mp, mw, mv, yp, yw, yv, rp, rw, rv,
    b1, b2, b3, b4, n4, w0, w1, w2, w3, w4, far,
    pick_t, acol, ycol,
    xwt, ywt, mwt, rwx, rwy, xwm, mwm,
    acc_x, acc_y, acc_xt, acc_mt, acc_rt,
    ret_m, ret_y, ret_r, in_m, in_y, in_r,
    back, home,
    send_sem, recv_sem, all_sem,
):
    me = lax.axis_index("leaf")
    chip = me // 2
    core = lax.rem(me, 2)
    mate = me + 1 - 2 * core
    here = lax.rem(me, GROUP)

    def at(offset, which=None):
        other = lax.rem(chip + offset + CHIPS, CHIPS)
        return other * 2 + (core if which is None else which)

    barrier = pltpu.get_barrier_semaphore()

    @pl.loop(1, LEAVES)
    def _(d):
        pl.semaphore_signal(
            barrier,
            inc=1,
            device_id=(lax.rem(me + d, LEAVES),),
            device_id_type=pl.DeviceIdType.MESH,
        )

    right, left = at(1), at(-1)
    copies = Copies(send_sem, recv_sem)
    quarter = [pl.ds(256 * i, 256) for i in range(4)]
    lane = iota((1, 128), 1)

    row = slot[...].astype(F32)
    rank = jnp.sum(jnp.where(column_of(row) < row, 1.0, 0.0), axis=0, keepdims=True)
    rank = rank.astype(jnp.int32)
    spot = jnp.bitwise_and(slot[...], N - 1)
    tail_s[...] = jnp.zeros_like(tail_s)
    tail_s[0:W, :] = weights_t[...].astype(F32)
    tail_s[W : W + 1, :] = jnp.right_shift(spot, 5).astype(F32)
    tail_s[W + 1 : W + 2, :] = jnp.bitwise_and(spot, 31).astype(F32)
    tail_in = jnp.transpose(tail_s[...]).astype(BF16)
    for i in range(4):
        pick = one_hot(iota((256, N), 0) + i * 256 == rank)
        rows = pl.ds(i * 32, 32)
        send[rows, :, 0:D] = dot(pick, points[...]).reshape(32, PEER, D).astype(BF16)
        send[rows, :, D:MESSAGE] = dot(pick, tail_in).reshape(32, PEER, 128).astype(BF16)
    lines[...] = jnp.zeros_like(lines)
    lines[0:1, 0:MERGE] = merge_i[...].astype(F32)
    merge_c = jnp.transpose(lines[...])[0:MERGE, 0:1].astype(jnp.int32)
    merge_h = jnp.right_shift(merge_c, 5).astype(F32)
    merge_l = jnp.bitwise_and(merge_c, 31).astype(F32)
    index[here] = jnp.where(lane == 0, merge_h, jnp.where(lane == 1, merge_l, 0.0)).astype(BF16)

    pl.semaphore_wait(barrier, LEAVES - 1)

    @pl.loop(1, LEAVES)
    def _(d):
        other = lax.rem(me + d, LEAVES)
        remote(send.at[other], came.at[me], all_sem.at[0], all_sem.at[1], other).start()

    indices = []
    for d in range(1, GROUP):
        first = 0 if d < 2 else 128 if d < 4 else 192 if d < 8 else 224
        rows = pl.ds(first, MERGE - first)
        indices.append(
            copies.start(index.at[here, rows], index.at[here, rows], me - here + jnp.bitwise_xor(here, d))
        )
    came[me] = send[me]
    skel_col = column_of(skel_row[...].astype(F32)).astype(jnp.int32)
    mask_row = jnp.zeros((1, N), F32)
    wide = iota((1, N), 1)
    for i in range(8):
        mask_row = jnp.where(wide == i, near_mask[0, i].astype(F32), mask_row)
    for i in range(16):
        mask_row = jnp.where(wide == 8 + i, far_mask[0, i // 4, i % 4].astype(F32), mask_row)
    for acc in (acc_x, acc_y, acc_xt, acc_mt, acc_rt):
        acc[...] = jnp.zeros_like(acc)
    everyone = remote(
        send.at[pl.ds(0, LEAVES - 1)], came.at[pl.ds(0, LEAVES - 1)], all_sem.at[0], all_sem.at[1], mate
    )
    everyone.wait_recv()

    for i in range(4):
        part = came[pl.ds(32 * i, 32)].astype(F32).reshape(256, MESSAGE)
        got[quarter[i], :] = part.astype(BF16)
        x = part[:, 0:D]
        acol[quarter[i], :] = (jnp.sum(x * x, axis=1, keepdims=True) - float(D)) * C_SHIFT
    to_right, to_left = [], []

    def send_quarter(i):
        src = got.at[quarter[i], pl.ds(0, D)]
        to_left.append(copies.start(src, rp.at[core, quarter[i]], left))
        to_right.append(copies.start(src, yp.at[quarter[i]], right))

    send_quarter(0)
    a_wide = jnp.broadcast_to(acol[...], (N, 128))
    xv[...] = jnp.where(iota((8, N), 0) == 0, jnp.transpose(a_wide)[0:8], mask_row)
    tail = got[:, D:MESSAGE].astype(F32)
    place = (tail[:, W : W + 1] * 32.0 + tail[:, W + 1 : W + 2]).astype(jnp.int32)
    tail_t = jnp.transpose(tail)
    place_row = (tail_t[W : W + 1] * 32.0 + tail_t[W + 1 : W + 2]).astype(jnp.int32)
    high = a_wide.astype(BF16).astype(F32)
    middle = (a_wide - high).astype(BF16).astype(F32)
    low = a_wide - high - middle
    aux = jnp.where(lane == W, high, jnp.where(lane == W + 1, middle, low))
    aux = jnp.where((lane >= W) & (lane < W + 3), aux, 0.0).astype(BF16)
    own_pick = one_hot(skel_col == place_row)
    b1[core, :, 0:D] = dot(own_pick, got[:, 0:D]).astype(BF16)
    b1[core, :, D:MESSAGE] = dot(own_pick, aux).astype(BF16)
    level0 = copies.start(b1.at[core], b1.at[core], mate)
    tree_w = dot(one_hot(iota((N, N), 0) == place_row), got[:, D:MESSAGE]).astype(BF16)
    own_w = pl.ds(pl.multiple_of(core * R, R), R)
    w0[own_w, :] = dot(interp[...], tree_w).astype(BF16)
    weight0 = copies.start(w0.at[own_w], w0.at[own_w], mate)
    mate_p = copies.start(got.at[:, pl.ds(0, D)], mp, mate)
    pick_t[...] = one_hot(place == skel_row[...])
    mwt[...] = jnp.where(iota((128, 1), 0) < W, tail_t, 0.0).astype(BF16)
    xwm[...] = jnp.where(lane < W, tail, 0.0).astype(BF16)

    def merge_points(level, children, store):
        rows = R >> level
        first = R - 2 * rows
        base = here - lax.rem(here, 1 << level)
        pieces = jnp.concatenate(
            [index[base + p, first : first + rows, :] for p in range(1 << level)], axis=0
        ).astype(F32)
        index_k = (pieces[:, 0:1] * 32.0 + pieces[:, 1:2]).astype(jnp.int32)
        chosen = one_hot(index_k == iota((R, 2 * R), 1))
        both = children[...].reshape(2 * R, MESSAGE)
        store[...] = dot(chosen, both).astype(BF16)
        return chosen

    def merge_weights(level, children, store):
        rows = R >> level
        first = R - 2 * rows
        span = min(2 << level, GROUP)
        mine = pl.ds(pl.multiple_of(lax.rem(here, span) * rows, rows), rows)
        store[mine, :] = dot(merge_w[first : first + rows, :], children[...]).astype(BF16)
        return [
            copies.start(
                store.at[mine], store.at[mine], me - here + jnp.bitwise_xor(here, d)
            )
            for d in range(1, span)
        ]

    def arrive(group):
        for copy in group:
            copy.wait_recv()

    half = pl.ds(pl.multiple_of(core * 128, 128), 128)
    even = lax.rem(chip, 2) == 0
    even4 = lax.rem(chip // 4, 2) == 0
    third, first = jnp.where(even, 3, 1), jnp.where(even, 1, 3)
    third4, first4 = jnp.where(even4, 12, 4), jnp.where(even4, 4, 12)
    targets = (
        (4, third, -first, -4),
        (8, 4, -4, -8),
        (16, third4, -first4, -16),
    )

    def send_far(level, node):
        return [
            copies.start(
                node.at[half, pl.ds(0, D)], far.at[4 * level + i, half, pl.ds(0, D)], at(targets[level][i])
            )
            for i in range(4)
        ]

    def send_far_tail(level, node):
        return [
            copies.start(
                node.at[:, pl.ds(D, 128)], far.at[4 * level + i, :, pl.ds(D, 128)], at(targets[level][i])
            )
            for i in range(4)
        ]

    def pass_on(copy, ref):
        copy.wait_recv()
        return copies.start(ref, ref, mate)

    def pass_far(slot):
        return pass_on(far_points[slot], far.at[slot, half, pl.ds(0, D)])

    def block(tp, ta, tw_t, sp, sa, sw, acc_t, acc_s):
        k = dot_nt(tp, sp) * C_DOT
        k = jnp.exp2(k - ta - sa).astype(BF16)
        if acc_t is not None:
            acc_t[...] += dot(k, sw)
        if acc_s is not None:
            acc_s[...] += dot(tw_t, k)

    def own_block(i):
        for j in range(i, 4):
            block(
                got[quarter[i], 0:D], acol[quarter[i], :], mwt[:, quarter[i]],
                got[quarter[j], 0:D], xv[0:1, quarter[j]], xwm[quarter[j], :],
                acc_x.at[quarter[i]], acc_xt.at[:, quarter[j]] if j > i else None,
            )

    own_block(0)

    arrive(indices)
    level0.wait_recv()
    side2 = lax.rem(chip, 2)
    chosen = merge_points(1, b1, b2.at[side2])
    level1 = copies.start(
        b2.at[side2, half], b2.at[side2, half], jnp.bitwise_xor(chip, 1) * 2 + core
    )
    weight0.wait_recv()
    weight1 = merge_weights(1, w0, w1)
    send_quarter(1)
    own_block(1)
    arrive(weight1)
    mine = jnp.where(core == 0, chosen[:, 0:R].astype(F32), chosen[:, R : 2 * R].astype(F32))
    placed = dot_nt(pick_t[...], mine.astype(BF16)).astype(BF16)
    tail1 = w1[pl.ds(pl.multiple_of(side2 * R, R), R), :]
    spread = pltpu.roll(dot(placed, tail1), W, 1)
    x_w = jnp.where(lane < W, tail, spread)
    xw[...] = x_w.astype(BF16)
    wv = []
    for src, dm, dl, dr in ((xw, mw, rw.at[core], yw), (xv, mv, rv.at[core], yv)):
        wv.append(
            (copies.start(src, dm, mate), copies.start(src, dl, left), copies.start(src, dr, right))
        )
    weight2 = merge_weights(2, w1, w2)

    level1.wait_recv()
    other2 = b2.at[1 - side2, half]
    shared = copies.start(other2, other2, mate)
    own_block(2)
    own_block(3)
    shared.wait_recv()
    side3 = lax.rem(chip // 2, 2)
    merge_points(2, b2, b3.at[side3])
    level2 = copies.start(
        b3.at[side3, half], b3.at[side3, half], jnp.bitwise_xor(chip, 3) * 2 + core
    )
    far_points = send_far(0, b3.at[side3])
    arrive(weight2)
    weight3 = merge_weights(3, w2, w3)
    send_quarter(2)

    mate_p.wait_recv()
    wv[0][0].wait_recv()
    wv[1][0].wait_recv()
    near_mate = pick_lane(xv[1:2, :], jnp.where(core == 0, 4, 3))
    mwm[...] = jnp.where(lane < W, mw[...].astype(F32) * near_mate, 0.0).astype(BF16)
    mwt[...] = (mwt[...].astype(F32) * near_mate).astype(BF16)

    def mate_block(h):
        for i in range(2):
            mine = pl.ds(h * 512 + i * 256, 256)
            theirs = pl.ds(pl.multiple_of(jnp.bitwise_xor(core, h) * 512, 512), 512)
            block(
                got[mine, 0:D], acol[mine, :], mwt[:, mine],
                mp[theirs, :], mv[0:1, theirs], mwm[theirs, :],
                acc_x.at[mine], acc_mt.at[:, theirs],
            )

    mate_block(0)
    passed_w = [pass_on(wv[0][1], rw.at[core]), pass_on(wv[1][1], rv.at[core])]
    passed_p = [pass_on(to_left[0], rp.at[core, quarter[0]])]
    mate_block(1)
    ret_m[...] = acc_mt[0:W, :]
    back_m = copies.start(ret_m, in_m, mate)
    level2.wait_recv()
    other3 = b3.at[1 - side3, half]
    shared = copies.start(other3, other3, mate)

    wv[0][2].wait_recv()
    wv[1][2].wait_recv()
    y_row = jnp.broadcast_to(yv[0:1, :], (8, N))
    ycol[...] = jnp.transpose(y_row)[:, 0:1]
    y_w = yw[...].astype(F32)
    y_t = jnp.transpose(y_w)
    x_t = jnp.transpose(xw[...].astype(F32))
    arrive(passed_w)
    low_lane = lane < W
    low_row = iota((128, 1), 0) < W
    x_mask, y_mask = xv[1:2, :], yv[1:2, :]
    for j in range(2):
        r_mask = rv[j, 1:2, :]
        r_w = rw[j].astype(F32)
        step = 2 + j - core
        near = pick_lane(x_mask, step + 3)
        rwx[j] = (r_w * jnp.where(low_lane, near, pick_lane(x_mask, 8 + 2))).astype(BF16)
        xwt[j] = (x_t * jnp.where(low_row, near, pick_lane(r_mask, 8 + 1))).astype(BF16)
        step = 4 + j - core
        near = jnp.where(step <= 4, pick_lane(y_mask, step + 3), 0.0)
        rwy[j] = (r_w * jnp.where(low_lane, near, pick_lane(y_mask, 8 + 3))).astype(BF16)
        ywt[j] = (y_t * jnp.where(low_row, near, pick_lane(r_mask, 8 + 0))).astype(BF16)

    def near_block(i, rows, tp, ta, tw_t, sw, acc):
        for j in range(2):
            block(
                tp[rows, 0:D], ta[rows, :], tw_t[j, :, rows],
                rp[j, i, :], rv[j, 0:1, i], sw[j, i, :],
                acc.at[rows], acc_rt.at[j, :, i],
            )

    def x_quarter(i):
        arrive([passed_p[i]])

        @pl.loop(0, 4)
        def _(t):
            rows = pl.ds(pl.multiple_of(t * 256, 256), 256)
            near_block(quarter[i], rows, got, acol, xwt, rwx, acc_x)

    def y_quarter(i):
        to_right[i].wait_recv()

        @pl.loop(0, i + 1)
        def _(t):
            rows = pl.ds(pl.multiple_of(t * 256, 256), 256)
            near_block(quarter[i], rows, yp, ycol, ywt, rwy, acc_y)

        @pl.loop(0, i)
        def _(t):
            rows = pl.ds(pl.multiple_of(t * 256, 256), 256)
            near_block(rows, quarter[i], yp, ycol, ywt, rwy, acc_y)

    x_quarter(0)
    shared.wait_recv()
    side4 = lax.rem(chip // 4, 2)
    merge_points(3, b3, b4.at[side4])
    level3 = copies.start(
        b4.at[side4, half], b4.at[side4, half], jnp.bitwise_xor(chip, 4) * 2 + core
    )
    far_points += send_far(1, b4.at[side4])
    arrive(weight3)
    weight4 = merge_weights(4, w3, w4)
    send_quarter(3)

    def with_weights(node, weights):
        node[:, D:MESSAGE] = jnp.where(
            lane < W, weights.astype(F32), node[:, D:MESSAGE].astype(F32)
        ).astype(BF16)

    y_quarter(0)
    passed_p.append(pass_on(to_left[1], rp.at[core, quarter[1]]))
    level3.wait_recv()
    other4 = b4.at[1 - side4, half]
    shared = copies.start(other4, other4, mate)
    x_quarter(1)
    shared.wait_recv()
    merge_points(4, b4, n4)
    far_points += send_far(2, n4)
    arrive(weight4)
    level1.wait_send()
    level2.wait_send()
    level3.wait_send()
    far_tails = []
    for level, node, weights in (
        (0, b3.at[side3], w2[pl.ds(pl.multiple_of(side3 * R, R), R), :]),
        (1, b4.at[side4], w3[pl.ds(pl.multiple_of(side4 * R, R), R), :]),
        (2, n4, w4[...]),
    ):
        with_weights(node, weights)
        far_tails += send_far_tail(level, node)
    y_quarter(1)
    passed_p.append(pass_on(to_left[2], rp.at[core, quarter[2]]))
    far_passed = [pass_far(slot) for slot in range(4)]
    x_quarter(2)
    y_quarter(2)
    passed_p.append(pass_on(to_left[3], rp.at[core, quarter[3]]))
    far_passed += [pass_far(slot) for slot in range(4, 8)]
    x_quarter(3)
    y_quarter(3)
    far_passed += [pass_far(slot) for slot in range(8, 12)]
    y_sum = acc_y[:, 0:W] + acc_y[:, W : 2 * W]
    ret_y[...] = jnp.transpose(jnp.concatenate([y_sum, y_sum], axis=1))[0:W]
    ret_r[...] = acc_rt[:, 0:W, :] + acc_rt[:, W : 2 * W, :]
    back_y = copies.start(ret_y, in_y, left)
    for j in range(2):
        copies.start(ret_r.at[j], in_r.at[core], at(1, j), COPIES - 2 + core)

    arrive(far_tails)
    arrive(far_passed)

    @pl.loop(0, 12)
    def _(slot):
        mask = pick_lane(x_mask, 12 + slot)
        f_tail = far[slot, :, D:MESSAGE].astype(F32)
        f_w = jnp.where(low_lane, f_tail * mask, 0.0).astype(BF16)
        f_t = jnp.transpose(f_tail)
        f_a = f_t[W : W + 1] + f_t[W + 1 : W + 2] + f_t[W + 2 : W + 3]
        f_p = far[slot, :, 0:D]
        for t in range(4):
            block(
                got[quarter[t], 0:D], acol[quarter[t], :], None,
                f_p, f_a, f_w, acc_x.at[quarter[t]], None,
            )

    back_m.wait_recv()
    back_y.wait_recv()
    for j in range(2):
        remote(
            ret_r.at[j], in_r.at[j], send_sem.at[COPIES - 1], recv_sem.at[COPIES - 2 + j], left
        ).wait_recv()
    total = acc_xt[0:W, :] + in_m[...] + in_y[...] + in_r[0] + in_r[1]
    total = jnp.transpose(jnp.concatenate([total, total], axis=0))
    x_sum = acc_x[...]
    total = total + x_sum + pltpu.roll(x_sum, W, 1)
    high = total.astype(BF16).astype(F32)
    total = jnp.where(lane < W, high, total - high)
    back[...] = total.reshape(LEAVES, PEER, 128).astype(BF16)

    @pl.loop(1, LEAVES)
    def _(d):
        other = lax.rem(me + d, LEAVES)
        remote(back.at[other], home.at[me], all_sem.at[2], all_sem.at[3], other).start()

    home[me] = back[me]
    everyone.wait_send()
    for copy in copies.all:
        if not any(copy is sent for sent in (level1, level2, level3)):
            copy.wait_send()
    row = slot[...].astype(F32)
    rank = jnp.sum(jnp.where(column_of(row) < row, 1.0, 0.0), axis=0, keepdims=True)
    rank = rank.astype(jnp.int32)
    returned = remote(
        back.at[pl.ds(0, LEAVES - 1)], home.at[pl.ds(0, LEAVES - 1)], all_sem.at[2], all_sem.at[3], mate
    )
    returned.wait_recv()
    home_t = jnp.transpose(home[...].astype(F32).reshape(N, 128)).astype(BF16)
    for i in range(4):
        pick = one_hot(iota((N, 256), 0) == rank[:, 256 * i : 256 * (i + 1)])
        both = dot(home_t, pick)
        out[:, quarter[i]] = both[0:W] + both[W : 2 * W]
    returned.wait_send()


def vmem(*shape, dtype=BF16):
    return pltpu.VMEM(shape, dtype)


def local(
    points, weights, tree_slot, leaf_interp, skel_leaf, merge_interp, merge_index, near_mask, far_mask
):
    in_vmem = pl.BlockSpec(memory_space=pltpu.VMEM)
    in_smem = pl.BlockSpec(memory_space=pltpu.SMEM)
    sums = pl.pallas_call(
        tree_kernel,
        out_shape=jax.ShapeDtypeStruct((W, N), F32),
        in_specs=[in_vmem] * 7 + [in_smem] * 2,
        out_specs=in_vmem,
        scratch_shapes=[
            vmem(LEAVES, PEER, MESSAGE), vmem(LEAVES, PEER, MESSAGE), vmem(N, MESSAGE),
            vmem(128, N, dtype=F32), vmem(GROUP, MERGE, 128), vmem(8, 256, dtype=F32),
            vmem(N, 128), vmem(8, N, dtype=F32),
            vmem(N, D), vmem(N, 128), vmem(8, N, dtype=F32),
            vmem(N, D), vmem(N, 128), vmem(8, N, dtype=F32),
            vmem(2, N, D), vmem(2, N, 128), vmem(2, 8, N, dtype=F32),
            vmem(2, R, MESSAGE), vmem(2, R, MESSAGE), vmem(2, R, MESSAGE), vmem(2, R, MESSAGE),
            vmem(R, MESSAGE),
            vmem(2 * R, 128), vmem(2 * R, 128), vmem(2 * R, 128), vmem(2 * R, 128), vmem(R, 128),
            vmem(12, R, MESSAGE),
            vmem(N, R), vmem(N, 1, dtype=F32), vmem(N, 1, dtype=F32),
            vmem(2, 128, N), vmem(2, 128, N), vmem(128, N),
            vmem(2, N, 128), vmem(2, N, 128), vmem(N, 128), vmem(N, 128),
            vmem(N, 128, dtype=F32), vmem(N, 128, dtype=F32),
            vmem(128, N, dtype=F32), vmem(128, N, dtype=F32), vmem(2, 128, N, dtype=F32),
            vmem(W, N, dtype=F32), vmem(W, N, dtype=F32), vmem(2, W, N, dtype=F32),
            vmem(W, N, dtype=F32), vmem(W, N, dtype=F32), vmem(2, W, N, dtype=F32),
            vmem(LEAVES, PEER, 128), vmem(LEAVES, PEER, 128),
            pltpu.SemaphoreType.DMA((COPIES,)), pltpu.SemaphoreType.DMA((COPIES,)),
            pltpu.SemaphoreType.DMA((4,)),
        ],
        compiler_params=pltpu.CompilerParams(
            collective_id=0, has_side_effects=True, vmem_limit_bytes=VMEM_LIMIT
        ),
        name="tree",
    )(
        tree_slot.reshape(1, N), weights.T, points, leaf_interp[0], skel_leaf, merge_interp[0],
        merge_index, near_mask, far_mask,
    )
    return sums.T


def solution(mesh):
    placed = (
        P("leaf", None),
        P("leaf", None),
        P("leaf"),
        P("leaf", None, None),
        P("leaf", None),
        P("leaf", None, None),
        P("leaf", None),
        P("leaf", None),
        P("leaf", None, None),
    )
    return jax.shard_map(
        local, mesh=mesh, in_specs=placed, out_specs=P("leaf", None), check_vma=False
    )
```

```python
import math

import jax
import jax.numpy as jnp
from jax import lax
from jax.experimental import pallas as pl
from jax.experimental.pallas import tpu as pltpu
from jax.sharding import PartitionSpec as P

D = 768
W = 64
N = 1024
R = 256
LEAVES = 128
CHIPS = 64
GROUP = 16
PEER = N // LEAVES
STRIDE = 37
MESSAGE = D + 128
MERGE = 240
F32 = jnp.float32
BF16 = jnp.bfloat16
SCALE = 1.0 / (1.75 * math.sqrt(D))
LOG2E = math.log2(math.e)
C_DOT = SCALE * LOG2E
C_SHIFT = 0.5 * SCALE * LOG2E
VMEM_LIMIT = 60 * 1024 * 1024


def iota(shape, dim):
    return lax.broadcasted_iota(jnp.int32, shape, dim)


def one_hot(hit):
    return jnp.where(hit, 1.0, 0.0).astype(BF16)


def dot(a, b):
    return jnp.dot(a, b, preferred_element_type=F32)


def dot_nt(a, b):
    return lax.dot_general(a, b, (((1,), (1,)), ((), ())), preferred_element_type=F32)


def remote(src, dst, send, recv, device):
    return pltpu.make_async_remote_copy(
        src_ref=src,
        dst_ref=dst,
        send_sem=send,
        recv_sem=recv,
        device_id=(device,),
        device_id_type=pl.DeviceIdType.MESH,
    )


class Copies:
    def __init__(self, send_sem, recv_sem):
        self.send_sem, self.recv_sem, self.all = send_sem, recv_sem, []

    def start(self, src, dst, device, recv=None):
        i = len(self.all)
        recv = i if recv is None else recv
        copy = remote(src, dst, self.send_sem.at[i], self.recv_sem.at[recv], device)
        copy.start()
        self.all.append(copy)
        return copy


COPIES = 160


def pick_lane(row, column):
    return jnp.sum(
        jnp.where(iota(row.shape, 1) == column, row, 0.0), axis=1, keepdims=True
    )


def column_of(row):
    return jnp.transpose(jnp.broadcast_to(row, (8, row.shape[1])))[:, 0:1]


def tree_kernel(
    slot, weights_t, points, interp, skel_row, merge_w, merge_i, near_mask, far_mask,
    out,
    send, came, got, tail_s, index, lines,
    xw, xv, mp, mw, mv, yp, yw, yv, rp, rw, rv,
    b1, b2, b3, b4, n4, w0, w1, w2, w3, w4, far,
    pick_t, acol, ycol,
    xwt, ywt, mwt, rwx, rwy, xwm, mwm,
    acc_x, acc_y, acc_xt, acc_mt, acc_rt,
    ret_m, ret_y, ret_r, in_m, in_y, in_r,
    back, home,
    send_sem, recv_sem, all_sem,
):
    me = lax.axis_index("leaf")
    chip = me // 2
    core = lax.rem(me, 2)
    mate = me + 1 - 2 * core
    here = lax.rem(me, GROUP)

    def at(offset, which=None):
        other = lax.rem(chip + offset + CHIPS, CHIPS)
        return other * 2 + (core if which is None else which)

    barrier = pltpu.get_barrier_semaphore()

    @pl.loop(1, LEAVES)
    def _(d):
        pl.semaphore_signal(
            barrier,
            inc=1,
            device_id=(lax.rem(me + d, LEAVES),),
            device_id_type=pl.DeviceIdType.MESH,
        )

    right, left = at(1), at(-1)
    copies = Copies(send_sem, recv_sem)
    quarter = [pl.ds(256 * i, 256) for i in range(4)]
    lane = iota((1, 128), 1)

    row = slot[...].astype(F32)
    rank = jnp.sum(jnp.where(column_of(row) < row, 1.0, 0.0), axis=0, keepdims=True)
    rank = rank.astype(jnp.int32)
    spot = jnp.bitwise_and(slot[...], N - 1)
    tail_s[...] = jnp.zeros_like(tail_s)
    tail_s[0:W, :] = weights_t[...].astype(F32)
    tail_s[W : W + 1, :] = jnp.right_shift(spot, 5).astype(F32)
    tail_s[W + 1 : W + 2, :] = jnp.bitwise_and(spot, 31).astype(F32)
    tail_in = jnp.transpose(tail_s[...]).astype(BF16)
    for i in range(4):
        pick = one_hot(iota((256, N), 0) + i * 256 == rank)
        rows = pl.ds(i * 32, 32)
        send[rows, :, 0:D] = dot(pick, points[...]).reshape(32, PEER, D).astype(BF16)
        send[rows, :, D:MESSAGE] = dot(pick, tail_in).reshape(32, PEER, 128).astype(BF16)
    lines[...] = jnp.zeros_like(lines)
    lines[0:1, 0:MERGE] = merge_i[...].astype(F32)
    merge_c = jnp.transpose(lines[...])[0:MERGE, 0:1].astype(jnp.int32)
    merge_h = jnp.right_shift(merge_c, 5).astype(F32)
    merge_l = jnp.bitwise_and(merge_c, 31).astype(F32)
    index[here] = jnp.where(lane == 0, merge_h, jnp.where(lane == 1, merge_l, 0.0)).astype(BF16)

    pl.semaphore_wait(barrier, LEAVES - 1)

    @pl.loop(1, LEAVES)
    def _(d):
        other = lax.rem(me + d * STRIDE, LEAVES)
        remote(send.at[other], came.at[me], all_sem.at[0], all_sem.at[1], other).start()

    indices = []
    for d in range(1, GROUP):
        first = 0 if d < 2 else 128 if d < 4 else 192 if d < 8 else 224
        rows = pl.ds(first, MERGE - first)
        indices.append(
            copies.start(index.at[here, rows], index.at[here, rows], me - here + jnp.bitwise_xor(here, d))
        )
    came[me] = send[me]
    skel_col = column_of(skel_row[...].astype(F32)).astype(jnp.int32)
    mask_row = jnp.zeros((1, N), F32)
    wide = iota((1, N), 1)
    for i in range(8):
        mask_row = jnp.where(wide == i, near_mask[0, i].astype(F32), mask_row)
    for i in range(16):
        mask_row = jnp.where(wide == 8 + i, far_mask[0, i // 4, i % 4].astype(F32), mask_row)
    for acc in (acc_x, acc_y, acc_xt, acc_mt, acc_rt):
        acc[...] = jnp.zeros_like(acc)
    everyone = remote(
        send.at[pl.ds(0, LEAVES - 1)], came.at[pl.ds(0, LEAVES - 1)], all_sem.at[0], all_sem.at[1], mate
    )
    everyone.wait_recv()

    for i in range(4):
        part = came[pl.ds(32 * i, 32)].astype(F32).reshape(256, MESSAGE)
        got[quarter[i], :] = part.astype(BF16)
        x = part[:, 0:D]
        acol[quarter[i], :] = (jnp.sum(x * x, axis=1, keepdims=True) - float(D)) * C_SHIFT
    to_right, to_left = [], []

    def send_quarter(i):
        src = got.at[quarter[i], pl.ds(0, D)]
        to_left.append(copies.start(src, rp.at[core, quarter[i]], left))
        to_right.append(copies.start(src, yp.at[quarter[i]], right))

    send_quarter(0)
    a_wide = jnp.broadcast_to(acol[...], (N, 128))
    xv[...] = jnp.where(iota((8, N), 0) == 0, jnp.transpose(a_wide)[0:8], mask_row)
    tail = got[:, D:MESSAGE].astype(F32)
    place = (tail[:, W : W + 1] * 32.0 + tail[:, W + 1 : W + 2]).astype(jnp.int32)
    tail_t = jnp.transpose(tail)
    place_row = (tail_t[W : W + 1] * 32.0 + tail_t[W + 1 : W + 2]).astype(jnp.int32)
    high = a_wide.astype(BF16).astype(F32)
    middle = (a_wide - high).astype(BF16).astype(F32)
    low = a_wide - high - middle
    aux = jnp.where(lane == W, high, jnp.where(lane == W + 1, middle, low))
    aux = jnp.where((lane >= W) & (lane < W + 3), aux, 0.0).astype(BF16)
    own_pick = one_hot(skel_col == place_row)
    b1[core, :, 0:D] = dot(own_pick, got[:, 0:D]).astype(BF16)
    b1[core, :, D:MESSAGE] = dot(own_pick, aux).astype(BF16)
    level0 = copies.start(b1.at[core], b1.at[core], mate)
    tree_w = dot(one_hot(iota((N, N), 0) == place_row), got[:, D:MESSAGE]).astype(BF16)
    own_w = pl.ds(pl.multiple_of(core * R, R), R)
    w0[own_w, :] = dot(interp[...], tree_w).astype(BF16)
    weight0 = copies.start(w0.at[own_w], w0.at[own_w], mate)
    mate_p = copies.start(got.at[:, pl.ds(0, D)], mp, mate)
    pick_t[...] = one_hot(place == skel_row[...])
    mwt[...] = jnp.where(iota((128, 1), 0) < W, tail_t, 0.0).astype(BF16)
    xwm[...] = jnp.where(lane < W, tail, 0.0).astype(BF16)

    def merge_points(level, children, store):
        rows = R >> level
        first = R - 2 * rows
        base = here - lax.rem(here, 1 << level)
        pieces = jnp.concatenate(
            [index[base + p, first : first + rows, :] for p in range(1 << level)], axis=0
        ).astype(F32)
        index_k = (pieces[:, 0:1] * 32.0 + pieces[:, 1:2]).astype(jnp.int32)
        chosen = one_hot(index_k == iota((R, 2 * R), 1))
        both = children[...].reshape(2 * R, MESSAGE)
        store[...] = dot(chosen, both).astype(BF16)
        return chosen

    def merge_weights(level, children, store):
        rows = R >> level
        first = R - 2 * rows
        span = min(2 << level, GROUP)
        mine = pl.ds(pl.multiple_of(lax.rem(here, span) * rows, rows), rows)
        store[mine, :] = dot(merge_w[first : first + rows, :], children[...]).astype(BF16)
        return [
            copies.start(
                store.at[mine], store.at[mine], me - here + jnp.bitwise_xor(here, d)
            )
            for d in range(1, span)
        ]

    def arrive(group):
        for copy in group:
            copy.wait_recv()

    half = pl.ds(pl.multiple_of(core * 128, 128), 128)
    even = lax.rem(chip, 2) == 0
    even4 = lax.rem(chip // 4, 2) == 0
    third, first = jnp.where(even, 3, 1), jnp.where(even, 1, 3)
    third4, first4 = jnp.where(even4, 12, 4), jnp.where(even4, 4, 12)
    targets = (
        (4, third, -first, -4),
        (8, 4, -4, -8),
        (16, third4, -first4, -16),
    )

    def send_far(level, node):
        return [
            copies.start(
                node.at[half, pl.ds(0, D)], far.at[4 * level + i, half, pl.ds(0, D)], at(targets[level][i])
            )
            for i in range(4)
        ]

    def send_far_tail(level, node):
        return [
            copies.start(
                node.at[:, pl.ds(D, 128)], far.at[4 * level + i, :, pl.ds(D, 128)], at(targets[level][i])
            )
            for i in range(4)
        ]

    def pass_on(copy, ref):
        copy.wait_recv()
        return copies.start(ref, ref, mate)

    def pass_far(slot):
        return pass_on(far_points[slot], far.at[slot, half, pl.ds(0, D)])

    def block(tp, ta, tw_t, sp, sa, sw, acc_t, acc_s):
        k = dot_nt(tp, sp) * C_DOT
        k = jnp.exp2(k - ta - sa).astype(BF16)
        if acc_t is not None:
            acc_t[...] += dot(k, sw)
        if acc_s is not None:
            acc_s[...] += dot(tw_t, k)

    def own_block(i):
        for j in range(i, 4):
            block(
                got[quarter[i], 0:D], acol[quarter[i], :], mwt[:, quarter[i]],
                got[quarter[j], 0:D], xv[0:1, quarter[j]], xwm[quarter[j], :],
                acc_x.at[quarter[i]], acc_xt.at[:, quarter[j]] if j > i else None,
            )

    own_block(0)

    arrive(indices)
    level0.wait_recv()
    side2 = lax.rem(chip, 2)
    chosen = merge_points(1, b1, b2.at[side2])
    level1 = copies.start(
        b2.at[side2, half], b2.at[side2, half], jnp.bitwise_xor(chip, 1) * 2 + core
    )
    weight0.wait_recv()
    weight1 = merge_weights(1, w0, w1)
    own_block(1)
    arrive(weight1)
    mine = jnp.where(core == 0, chosen[:, 0:R].astype(F32), chosen[:, R : 2 * R].astype(F32))
    placed = dot_nt(pick_t[...], mine.astype(BF16)).astype(BF16)
    tail1 = w1[pl.ds(pl.multiple_of(side2 * R, R), R), :]
    spread = pltpu.roll(dot(placed, tail1), W, 1)
    x_w = jnp.where(lane < W, tail, spread)
    xw[...] = x_w.astype(BF16)
    wv = []
    for src, dm, dl, dr in ((xw, mw, rw.at[core], yw), (xv, mv, rv.at[core], yv)):
        wv.append(
            (copies.start(src, dm, mate), copies.start(src, dl, left), copies.start(src, dr, right))
        )
    weight2 = merge_weights(2, w1, w2)

    level1.wait_recv()
    other2 = b2.at[1 - side2, half]
    shared = copies.start(other2, other2, mate)
    own_block(2)
    own_block(3)
    shared.wait_recv()
    side3 = lax.rem(chip // 2, 2)
    merge_points(2, b2, b3.at[side3])
    level2 = copies.start(
        b3.at[side3, half], b3.at[side3, half], jnp.bitwise_xor(chip, 3) * 2 + core
    )
    far_points = send_far(0, b3.at[side3])
    arrive(weight2)
    weight3 = merge_weights(3, w2, w3)
    send_quarter(1)

    mate_p.wait_recv()
    wv[0][0].wait_recv()
    wv[1][0].wait_recv()
    near_mate = pick_lane(xv[1:2, :], jnp.where(core == 0, 4, 3))
    mwm[...] = jnp.where(lane < W, mw[...].astype(F32) * near_mate, 0.0).astype(BF16)
    mwt[...] = (mwt[...].astype(F32) * near_mate).astype(BF16)

    def mate_block(h):
        for i in range(2):
            mine = pl.ds(h * 512 + i * 256, 256)
            theirs = pl.ds(pl.multiple_of(jnp.bitwise_xor(core, h) * 512, 512), 512)
            block(
                got[mine, 0:D], acol[mine, :], mwt[:, mine],
                mp[theirs, :], mv[0:1, theirs], mwm[theirs, :],
                acc_x.at[mine], acc_mt.at[:, theirs],
            )

    mate_block(0)
    passed_w = [pass_on(wv[0][1], rw.at[core]), pass_on(wv[1][1], rv.at[core])]
    passed_p = [pass_on(to_left[0], rp.at[core, quarter[0]])]
    mate_block(1)
    ret_m[...] = acc_mt[0:W, :]
    back_m = copies.start(ret_m, in_m, mate)
    level2.wait_recv()
    other3 = b3.at[1 - side3, half]
    shared = copies.start(other3, other3, mate)

    wv[0][2].wait_recv()
    wv[1][2].wait_recv()
    y_row = jnp.broadcast_to(yv[0:1, :], (8, N))
    ycol[...] = jnp.transpose(y_row)[:, 0:1]
    y_w = yw[...].astype(F32)
    y_t = jnp.transpose(y_w)
    x_t = jnp.transpose(xw[...].astype(F32))
    arrive(passed_w)
    low_lane = lane < W
    low_row = iota((128, 1), 0) < W
    x_mask, y_mask = xv[1:2, :], yv[1:2, :]
    for j in range(2):
        r_mask = rv[j, 1:2, :]
        r_w = rw[j].astype(F32)
        step = 2 + j - core
        near = pick_lane(x_mask, step + 3)
        rwx[j] = (r_w * jnp.where(low_lane, near, pick_lane(x_mask, 8 + 2))).astype(BF16)
        xwt[j] = (x_t * jnp.where(low_row, near, pick_lane(r_mask, 8 + 1))).astype(BF16)
        step = 4 + j - core
        near = jnp.where(step <= 4, pick_lane(y_mask, step + 3), 0.0)
        rwy[j] = (r_w * jnp.where(low_lane, near, pick_lane(y_mask, 8 + 3))).astype(BF16)
        ywt[j] = (y_t * jnp.where(low_row, near, pick_lane(r_mask, 8 + 0))).astype(BF16)

    def near_block(i, rows, tp, ta, tw_t, sw, acc):
        for j in range(2):
            block(
                tp[rows, 0:D], ta[rows, :], tw_t[j, :, rows],
                rp[j, i, :], rv[j, 0:1, i], sw[j, i, :],
                acc.at[rows], acc_rt.at[j, :, i],
            )

    def x_quarter(i):
        arrive([passed_p[i]])
        for rows in quarter:
            near_block(quarter[i], rows, got, acol, xwt, rwx, acc_x)

    def y_quarter(i):
        to_right[i].wait_recv()
        for rows in quarter[: i + 1]:
            near_block(quarter[i], rows, yp, ycol, ywt, rwy, acc_y)
        for rows in quarter[:i]:
            near_block(rows, quarter[i], yp, ycol, ywt, rwy, acc_y)

    def far_level(level):
        arrive(far_tails[4 * level : 4 * level + 4])
        arrive(far_passed[4 * level : 4 * level + 4])
        for first_slot in (4 * level, 4 * level + 2):
            f_p, f_a, f_w = [], [], []
            for slot in (first_slot, first_slot + 1):
                f_tail = far[slot, :, D:MESSAGE].astype(F32)
                f_w.append(jnp.where(low_lane, f_tail * pick_lane(x_mask, 12 + slot), 0.0))
                f_t = jnp.transpose(f_tail)
                f_a.append(f_t[W : W + 1] + f_t[W + 1 : W + 2] + f_t[W + 2 : W + 3])
                f_p.append(far[slot, :, 0:D])
            f_p = jnp.concatenate(f_p, axis=0)
            f_a = jnp.concatenate(f_a, axis=1)
            f_w = jnp.concatenate(f_w, axis=0).astype(BF16)
            for rows in quarter:
                block(
                    got[rows, 0:D], acol[rows, :], None, f_p, f_a, f_w, acc_x.at[rows], None
                )

    shared.wait_recv()
    side4 = lax.rem(chip // 4, 2)
    merge_points(3, b3, b4.at[side4])
    level3 = copies.start(
        b4.at[side4, half], b4.at[side4, half], jnp.bitwise_xor(chip, 4) * 2 + core
    )
    far_points += send_far(1, b4.at[side4])
    arrive(weight3)
    weight4 = merge_weights(4, w3, w4)
    send_quarter(2)
    send_quarter(3)
    x_quarter(0)

    def with_weights(node, weights):
        node[:, D:MESSAGE] = jnp.where(
            lane < W, weights.astype(F32), node[:, D:MESSAGE].astype(F32)
        ).astype(BF16)

    level3.wait_recv()
    other4 = b4.at[1 - side4, half]
    shared = copies.start(other4, other4, mate)
    passed_p.append(pass_on(to_left[1], rp.at[core, quarter[1]]))
    y_quarter(0)
    shared.wait_recv()
    merge_points(4, b4, n4)
    far_points += send_far(2, n4)
    arrive(weight4)
    level1.wait_send()
    level2.wait_send()
    level3.wait_send()
    far_tails = []
    for level, node, weights in (
        (0, b3.at[side3], w2[pl.ds(pl.multiple_of(side3 * R, R), R), :]),
        (1, b4.at[side4], w3[pl.ds(pl.multiple_of(side4 * R, R), R), :]),
        (2, n4, w4[...]),
    ):
        with_weights(node, weights)
        far_tails += send_far_tail(level, node)
    x_quarter(1)
    passed_p.append(pass_on(to_left[2], rp.at[core, quarter[2]]))
    y_quarter(1)
    x_quarter(2)
    far_passed = [pass_far(slot) for slot in range(4)]
    y_quarter(2)
    far_level(0)
    passed_p.append(pass_on(to_left[3], rp.at[core, quarter[3]]))
    far_passed += [pass_far(slot) for slot in range(4, 8)]
    x_quarter(3)
    y_quarter(3)
    y_sum = acc_y[:, 0:W] + acc_y[:, W : 2 * W]
    ret_y[...] = jnp.transpose(jnp.concatenate([y_sum, y_sum], axis=1))[0:W].astype(BF16)
    ret_r[...] = (acc_rt[:, 0:W, :] + acc_rt[:, W : 2 * W, :]).astype(BF16)
    back_y = copies.start(ret_y, in_y, left)
    for j in range(2):
        copies.start(ret_r.at[j], in_r.at[core], at(1, j), COPIES - 2 + core)

    far_passed += [pass_far(slot) for slot in range(8, 12)]
    far_level(1)
    far_level(2)
    back_m.wait_recv()
    back_y.wait_recv()
    for j in range(2):
        remote(
            ret_r.at[j], in_r.at[j], send_sem.at[COPIES - 1], recv_sem.at[COPIES - 2 + j], left
        ).wait_recv()
    total = acc_xt[0:W, :] + in_m[...] + in_y[...].astype(F32)
    total = total + in_r[0].astype(F32) + in_r[1].astype(F32)
    total = jnp.transpose(jnp.concatenate([total, total], axis=0))
    x_sum = acc_x[...]
    total = total + x_sum + pltpu.roll(x_sum, W, 1)
    high = total.astype(BF16).astype(F32)
    total = jnp.where(lane < W, high, total - high)
    back[...] = total.reshape(LEAVES, PEER, 128).astype(BF16)

    @pl.loop(1, LEAVES)
    def _(d):
        other = lax.rem(me + d * STRIDE, LEAVES)
        remote(back.at[other], home.at[me], all_sem.at[2], all_sem.at[3], other).start()

    home[me] = back[me]
    everyone.wait_send()
    for copy in copies.all:
        if not any(copy is sent for sent in (level1, level2, level3)):
            copy.wait_send()
    row = slot[...].astype(F32)
    rank = jnp.sum(jnp.where(column_of(row) < row, 1.0, 0.0), axis=0, keepdims=True)
    rank = rank.astype(jnp.int32)
    returned = remote(
        back.at[pl.ds(0, LEAVES - 1)], home.at[pl.ds(0, LEAVES - 1)], all_sem.at[2], all_sem.at[3], mate
    )
    returned.wait_recv()
    home_t = jnp.transpose(home[...].astype(F32).reshape(N, 128)).astype(BF16)
    for i in range(4):
        pick = one_hot(iota((N, 256), 0) == rank[:, 256 * i : 256 * (i + 1)])
        both = dot(home_t, pick)
        out[:, quarter[i]] = both[0:W] + both[W : 2 * W]
    returned.wait_send()


def vmem(*shape, dtype=BF16):
    return pltpu.VMEM(shape, dtype)


def local(
    points, weights, tree_slot, leaf_interp, skel_leaf, merge_interp, merge_index, near_mask, far_mask
):
    in_vmem = pl.BlockSpec(memory_space=pltpu.VMEM)
    in_smem = pl.BlockSpec(memory_space=pltpu.SMEM)
    sums = pl.pallas_call(
        tree_kernel,
        out_shape=jax.ShapeDtypeStruct((W, N), F32),
        in_specs=[in_vmem] * 7 + [in_smem] * 2,
        out_specs=in_vmem,
        scratch_shapes=[
            vmem(LEAVES, PEER, MESSAGE), vmem(LEAVES, PEER, MESSAGE), vmem(N, MESSAGE),
            vmem(128, N, dtype=F32), vmem(GROUP, MERGE, 128), vmem(8, 256, dtype=F32),
            vmem(N, 128), vmem(8, N, dtype=F32),
            vmem(N, D), vmem(N, 128), vmem(8, N, dtype=F32),
            vmem(N, D), vmem(N, 128), vmem(8, N, dtype=F32),
            vmem(2, N, D), vmem(2, N, 128), vmem(2, 8, N, dtype=F32),
            vmem(2, R, MESSAGE), vmem(2, R, MESSAGE), vmem(2, R, MESSAGE), vmem(2, R, MESSAGE),
            vmem(R, MESSAGE),
            vmem(2 * R, 128), vmem(2 * R, 128), vmem(2 * R, 128), vmem(2 * R, 128), vmem(R, 128),
            vmem(12, R, MESSAGE),
            vmem(N, R), vmem(N, 1, dtype=F32), vmem(N, 1, dtype=F32),
            vmem(2, 128, N), vmem(2, 128, N), vmem(128, N),
            vmem(2, N, 128), vmem(2, N, 128), vmem(N, 128), vmem(N, 128),
            vmem(N, 128, dtype=F32), vmem(N, 128, dtype=F32),
            vmem(128, N, dtype=F32), vmem(128, N, dtype=F32), vmem(2, 128, N, dtype=F32),
            vmem(W, N, dtype=F32), vmem(W, N), vmem(2, W, N),
            vmem(W, N, dtype=F32), vmem(W, N), vmem(2, W, N),
            vmem(LEAVES, PEER, 128), vmem(LEAVES, PEER, 128),
            pltpu.SemaphoreType.DMA((COPIES,)), pltpu.SemaphoreType.DMA((COPIES,)),
            pltpu.SemaphoreType.DMA((4,)),
        ],
        compiler_params=pltpu.CompilerParams(
            collective_id=0, has_side_effects=True, vmem_limit_bytes=VMEM_LIMIT
        ),
        name="tree",
    )(
        tree_slot.reshape(1, N), weights.T, points, leaf_interp[0], skel_leaf, merge_interp[0],
        merge_index, near_mask, far_mask,
    )
    return sums.T


def solution(mesh):
    placed = (
        P("leaf", None),
        P("leaf", None),
        P("leaf"),
        P("leaf", None, None),
        P("leaf", None),
        P("leaf", None, None),
        P("leaf", None),
        P("leaf", None),
        P("leaf", None, None),
    )
    return jax.shard_map(
        local, mesh=mesh, in_specs=placed, out_specs=P("leaf", None), check_vma=False
    )
```
